256 devices in a mesh: row: 8 (over x, core), col: 32 (over y, z).
Axes of the slice: x: 4, y: 4, z: 8, core: 2. Of those that a mesh axis runs over, the one named last changes fastest.
Arguments:
- matrix: float32 [16384, 16384], P('row', 'col'), as said below
- panel: float32 [16384, 256], P(('row', 'col')), may hold values from -0.046875 to 0.046875
- factor: float32 [256, 256], replicated, as said below
Outputs:
- updated: float32 [16384, 16384], P('row', 'col')
- correction: float32 [16384, 256], P(('row', 'col'))
The draws below stay inside these ranges and needn't reach their ends.
Inputs may be any that keep to these rules, and one draw needn't show every extreme that they name: `matrix`: symmetric. `factor`: upper triangular with a positive diagonal.
All inputs are finite; a program needn't handle non-finite values.
Results may differ from the reference program's by a relative error of at most 0.000071.
Values sent between devices are 32-bit elements; how exact they have to be, the bound alone decides.
No kernel may reach another device: no remote copies, remote signals or barrier semaphores. Data moves between devices by JAX's collectives and lax.ppermute only.
A program may use at most 64 MiB of HBM per device.

```python
import math
import jax
import jax.numpy as jnp
from jax import lax

B = 256
N = 16384


def draw_matrix(key, part):
    noise = jax.random.normal(key, (N, N), jnp.float32)
    return (noise + noise.T) * 0.70710678


def draw_factor(key, part):
    upper = jax.random.normal(jax.random.fold_in(key, 3), (B, B), jnp.float32) * (0.5 / math.sqrt(B))
    diag_vals = jax.random.uniform(jax.random.fold_in(key, 5), (B,), jnp.float32, 0.6, 1.4)
    return jnp.triu(upper, 1) + jnp.diag(diag_vals)


def level_of(stream_key, dims, shards, smallest, high):
    loudness, own = 1.0, jax.random.fold_in(stream_key, 6)
    for dim, shards_of in shards:
        heights = jnp.exp(jax.random.uniform(jax.random.fold_in(own, dim), (shards_of,), jnp.float32, smallest / len(shards), high / len(shards)))
        loudness = loudness * jnp.repeat(heights, dims[dim] // shards_of).reshape([-1 if axis == dim else 1 for axis in range(len(dims))])
    return loudness


def bell_draw(rng, dims, width, limit, pieces=(), dtype=jnp.bfloat16):
    values = jax.random.normal(rng, dims, jnp.float32) * width
    if len(pieces) > 0:
        values = level_of(rng, dims, pieces, -0.22, 0.18) * values
    return jnp.clip(values, min=-limit, max=limit).astype(dtype)


def setup_inputs(seed: int = 0) -> dict:
    keys = jax.random.split(jax.random.key(seed), 4)
    return {
        "matrix": draw_matrix(jax.random.fold_in(keys[3], 71), 0),
        "panel": bell_draw(keys[1], (N, B), N ** -0.5, 0.046875, ((0, 256),), jnp.float32),
        "factor": draw_factor(jax.random.fold_in(keys[3], 71), 0),
    }


def mult(left, right):
    return jnp.dot(left, right, precision=lax.Precision.HIGHEST, preferred_element_type=jnp.float32)


def reference(matrix, panel, factor):
    product = mult(matrix, panel)
    scaled = mult(product, factor)
    small = mult(panel.T, scaled)
    correction = scaled - 0.5 * mult(panel, mult(factor.T, small))
    updated = matrix - mult(panel, correction.T) - mult(correction, panel.T)
    return updated, correction
```

```python
import jax
import jax.numpy as jnp
from jax import lax
from jax.sharding import PartitionSpec as P

NY, NZ = 4, 8
HIGH = lax.Precision.HIGH
Z_GROUPS = [[y * NZ + z for z in range(NZ)] for y in range(NY)]
Y_GROUPS = [[y * NZ + z for y in range(NY)] for z in range(NZ)]


def dot(left, right, contract):
    return lax.dot_general(
        left, right, (contract, ((), ())), precision=HIGH, preferred_element_type=jnp.float32
    )


def spread(value, groups):
    count = len(groups[0])
    copies = jnp.broadcast_to(value, (count,) + value.shape)
    return lax.all_to_all(copies, "col", 0, 0, axis_index_groups=groups)


def y_shift(value, step):
    perm = [(y * NZ + z, (y + step) % NY * NZ + z) for y in range(NY) for z in range(NZ)]
    return lax.ppermute(value, "col", perm)


def home_to_column(nrows):
    pairs = []
    for r in range(nrows):
        for y in range(NY):
            for z in range(NZ):
                block = y * NZ + z
                pairs.append(((block // NY * NY + block % NY) * NZ + r, r * NY * NZ + block))
    return pairs


def per_device(matrix, panel, factor):
    nrows = lax.axis_size("row")
    rows, width = panel.shape
    block = rows * NZ
    row, col = lax.axis_index("row"), lax.axis_index("col")
    y, z = col // NZ, col % NZ
    to_column = home_to_column(nrows)
    to_home = [(b, a) for a, b in to_column]

    own_block = spread(panel, Z_GROUPS).reshape(block, width)
    col_panel = lax.ppermute(own_block, ("row", "col"), to_column)
    row_panel = spread(own_block, Y_GROUPS).reshape(block * NY, width)

    partial = dot(matrix, row_panel, ((0,), (0,)))
    partial = dot(partial, factor, ((1,), (0,)))
    parts = lax.all_to_all(partial.reshape(nrows, rows, width), "row", 0, 0)
    chunk = jnp.sum(parts, axis=0)
    col_scaled = lax.all_gather(chunk, "row", axis=0, tiled=True)

    home = lax.ppermute(col_scaled, ("row", "col"), to_home)
    others = [y_shift(home, step) for step in (1, 2, 3)]
    inner = dot(col_panel, col_scaled, ((0,), (0,)))
    depth = width // nrows
    inner = lax.dynamic_slice_in_dim(inner, row * depth, depth, 0)
    inner = jnp.sum(spread(inner, Z_GROUPS), axis=0)
    inner = jnp.sum(spread(inner, Y_GROUPS), axis=0)
    small = lax.all_gather(inner, "row", axis=0, tiled=True)
    kernel = 0.5 * dot(factor, small, ((0,), (0,)))

    scaled = lax.dynamic_slice_in_dim(home, z * rows, rows, 0)
    correction = scaled - dot(panel, kernel, ((1,), (0,)))
    left = col_scaled - dot(col_panel, kernel + kernel.T, ((1,), (0,)))
    stacked = jnp.stack([home, others[2], others[1], others[0]])
    row_scaled = jnp.roll(stacked, y, axis=0).reshape(block * NY, width)
    updated = (
        matrix
        - dot(row_panel, left, ((1,), (1,)))
        - dot(row_scaled, col_panel, ((1,), (1,)))
    )
    return updated, correction


def solution(mesh):
    in_specs = (P("row", "col"), P(("row", "col"), None), P())
    out_specs = (P("row", "col"), P(("row", "col"), None))
    return jax.shard_map(
        per_device, mesh=mesh, in_specs=in_specs, out_specs=out_specs, check_vma=False
    )
```

```python
import jax
import jax.numpy as jnp
from jax import lax
from jax.experimental import pallas as pl
from jax.experimental.pallas import tpu as pltpu
from jax.sharding import PartitionSpec as P

NY, NZ = 4, 8
HIGH = lax.Precision.HIGH
Z_GROUPS = [[y * NZ + z for z in range(NZ)] for y in range(NY)]
Y_GROUPS = [[y * NZ + z for y in range(NY)] for z in range(NZ)]
TILE = 256


def dot(left, right, contract):
    return lax.dot_general(
        left, right, (contract, ((), ())), precision=HIGH, preferred_element_type=jnp.float32
    )


def spread(value, axis, groups=None):
    count = lax.axis_size(axis) if groups is None else len(groups[0])
    copies = jnp.broadcast_to(value, (count,) + value.shape)
    return lax.all_to_all(copies, axis, 0, 0, axis_index_groups=groups)


def y_shift(value, step):
    perm = [(y * NZ + z, (y + step) % NY * NZ + z) for y in range(NY) for z in range(NZ)]
    return lax.ppermute(value, "col", perm)


def y_blocks(value):
    return [value] + [y_shift(value, step) for step in range(1, NY)]


def after(value, *others):
    return lax.optimization_barrier((value,) + others)[0]


def halves(value):
    high = value.astype(jnp.bfloat16)
    return high, (value - high.astype(jnp.float32)).astype(jnp.bfloat16)


def update_kernel(y_ref, matrix, right, *refs):
    panels, scaleds = refs[:NY], refs[NY : 2 * NY]
    out, left, right_high, right_low = refs[2 * NY :]
    step = pl.program_id(0)

    @pl.when((step == 0) & (pl.program_id(1) == 0))
    def _():
        right_high[...], right_low[...] = halves(right[...])

    width = left.shape[1] // 2
    for k in range(NY):

        @pl.when(step == k)
        def _():
            left[:, :width] = panels[k][...]
            left[:, width:] = scaleds[k][...]

    left_high, left_low = halves(left[...])
    total = jnp.dot(left_high, right_low[...], preferred_element_type=jnp.float32)
    total += jnp.dot(left_low, right_high[...], preferred_element_type=jnp.float32)
    total += jnp.dot(left_high, right_high[...], preferred_element_type=jnp.float32)
    out[...] = matrix[...] - total


def update(y, matrix, panels, scaleds, right):
    rows, cols = matrix.shape
    block, width = panels[0].shape
    tiles = block // TILE

    def moving(s, h, y_ref):
        return (lax.rem(y_ref[0] + (NY - s), NY) * tiles + h, 0)

    def part(k):
        def index(s, h, y_ref):
            return (jnp.where(s == k, h, jnp.where(s < k, 0, tiles - 1)), 0)

        return pl.BlockSpec((TILE, width), index)

    parts = [part(k) for k in range(NY)]
    return pl.pallas_call(
        update_kernel,
        out_shape=jax.ShapeDtypeStruct((rows, cols), jnp.float32),
        grid_spec=pltpu.PrefetchScalarGridSpec(
            num_scalar_prefetch=1,
            grid=(NY, tiles),
            in_specs=[
                pl.BlockSpec((TILE, cols), moving),
                pl.BlockSpec((2 * width, cols), lambda s, h, y_ref: (0, 0)),
            ]
            + parts
            + parts,
            out_specs=pl.BlockSpec((TILE, cols), moving),
            scratch_shapes=[
                pltpu.VMEM((TILE, 2 * width), jnp.float32),
                pltpu.VMEM((2 * width, cols), jnp.bfloat16),
                pltpu.VMEM((2 * width, cols), jnp.bfloat16),
            ],
        ),
        cost_estimate=pl.CostEstimate(
            flops=12 * rows * cols * width,
            bytes_accessed=8 * rows * cols + 8 * rows * width,
            transcendentals=0,
        ),
        compiler_params=pltpu.CompilerParams(vmem_limit_bytes=24 << 20),
    )(y.reshape(1), matrix, right, *panels, *scaleds)


def per_device(matrix, panel, factor):
    nrows, ncols = lax.axis_size("row"), lax.axis_size("col")
    rows, width = panel.shape
    block = NZ * rows
    depth = width // nrows
    y = lax.axis_index("col") // NZ
    total = nrows * ncols
    to_column = [(g, g % nrows * ncols + g // nrows) for g in range(total)]
    to_home = [(b, a) for a, b in to_column]

    moved = lax.ppermute(panel, ("row", "col"), to_column)
    own_panel = spread(panel, "col", Z_GROUPS).reshape(block, width)
    panels = y_blocks(own_panel)
    col_panel = spread(after(moved, own_panel), "row").reshape(nrows * rows, width)

    partial = 0.0
    for step in range(NY):
        start = lax.rem(y + (NY - step), NY) * block
        piece = lax.dynamic_slice_in_dim(matrix, start, block, 0)
        partial += dot(piece, panels[step], ((0,), (0,)))
    partial = dot(partial, factor, ((1,), (0,)))
    inner = dot(col_panel, partial, ((0,), (0,)))
    parts = jnp.concatenate(
        [partial.reshape(nrows, rows, width), inner.reshape(nrows, depth, width)], axis=1
    )
    parts = jnp.sum(lax.all_to_all(parts, "row", 0, 0), axis=0)
    chunk, inner = parts[:rows], parts[rows:]

    home = lax.ppermute(chunk, ("row", "col"), to_home)
    inner = jnp.sum(spread(inner, "col", Z_GROUPS), axis=0)
    own_scaled = spread(after(home, inner), "col", Z_GROUPS).reshape(block, width)
    inner = sum(y_blocks(inner))
    scaleds = y_blocks(own_scaled)
    gathered = spread(after(jnp.concatenate([chunk, inner]), own_scaled), "row")
    col_scaled = gathered[:, :rows].reshape(nrows * rows, width)
    small = gathered[:, rows:].reshape(width, width)

    kernel = 0.5 * dot(factor, small, ((0,), (0,)))
    correction = home - dot(panel, kernel, ((1,), (0,)))
    left = col_scaled - dot(col_panel, kernel + kernel.T, ((1,), (0,)))
    right = jnp.concatenate([left.T, col_panel.T], axis=0)
    return update(y, matrix, panels, scaleds, right), correction


def solution(mesh):
    in_specs = (P("row", "col"), P(("row", "col"), None), P())
    out_specs = (P("row", "col"), P(("row", "col"), None))
    return jax.shard_map(
        per_device, mesh=mesh, in_specs=in_specs, out_specs=out_specs, check_vma=False
    )
```

```python
import jax
import jax.numpy as jnp
from jax import lax
from jax.experimental import pallas as pl
from jax.experimental.pallas import tpu as pltpu
from jax.sharding import PartitionSpec as P

NX, NY, NZ, CORES = 4, 4, 8, 2
Z_GROUPS = [[y * NZ + z for z in range(NZ)] for y in range(NY)]
WHOLE = pl.BlockSpec(memory_space=pltpu.VMEM)
SCALARS = pl.BlockSpec(memory_space=pltpu.SMEM)
FREE = pl.CostEstimate(flops=1, bytes_accessed=1, transcendentals=0)
PARAMS = pltpu.CompilerParams(vmem_limit_bytes=28 << 20)


def after(value, *others):
    return lax.optimization_barrier((value,) + others)[0]


def exact(left, right, contract):
    return lax.dot_general(
        left,
        right,
        (contract, ((), ())),
        precision=lax.Precision.HIGHEST,
        preferred_element_type=jnp.float32,
    )


def halves(value):
    high = value.astype(jnp.bfloat16)
    return high, (value - high.astype(jnp.float32)).astype(jnp.bfloat16)


def three_pass(left, right, contract):
    def one(a, b):
        return lax.dot_general(a, b, (contract, ((), ())), preferred_element_type=jnp.float32)

    return one(left[0], right[1]) + one(left[1], right[0]) + one(left[0], right[0])


def spread(value, groups):
    copies = jnp.broadcast_to(value, (len(groups[0]),) + value.shape)
    return lax.all_to_all(copies, "col", 0, 0, axis_index_groups=groups)


def y_blocks(value):
    def shifted(step):
        perm = [(y * NZ + z, (y + step) % NY * NZ + z) for y in range(NY) for z in range(NZ)]
        return lax.ppermute(value, "col", perm)

    return [value] + [shifted(step) for step in range(1, NY)]


def z_sum(value):
    bit = 1
    while bit < NZ:
        perm = [(y * NZ + z, y * NZ + (z ^ bit)) for y in range(NY) for z in range(NZ)]
        value += lax.ppermute(value, "col", perm)
        bit *= 2
    return value


def x_blocks(value):
    size = NX * CORES

    def shifted(step):
        perm = [(i, (i - CORES * step) % size) for i in range(size)]
        return lax.ppermute(value, "row", perm)

    return [value] + [shifted(step) for step in range(1, NX)]


def other_core(values):
    perm = [(i, i ^ 1) for i in range(NX * CORES)]
    return lax.ppermute(jnp.stack(values), "row", perm)


def assemble(place, mine, other, out):
    for k in range(NX):
        slot = lax.rem(place[0] + k, NX) * CORES
        out[slot + place[1]] = mine[k][...]
        out[slot + 1 - place[1]] = other[k]


def assemble_kernel(place, *refs):
    assemble(place, refs[:NX], refs[NX], refs[NX + 1])


def row_blocks(place, mine, other):
    shape = (NX * CORES,) + mine[0].shape
    return pl.pallas_call(
        assemble_kernel,
        out_shape=jax.ShapeDtypeStruct(shape, mine[0].dtype),
        in_specs=[SCALARS] + [WHOLE] * (NX + 1),
        out_specs=WHOLE,
        cost_estimate=FREE,
        compiler_params=PARAMS,
    )(place, *mine, other)


def product_kernel(y_ref, matrix, factor, col_panel, *refs):
    panels, out, total = refs[:NY], refs[NY], refs[NY + 1]
    step = pl.program_id(0)
    for k in range(NY):

        @pl.when(step == k)
        def _():
            piece = three_pass(halves(panels[k][...]), halves(matrix[...]), ((0,), (0,)))
            if k == 0:
                total[...] = piece
            else:
                total[...] += piece

    @pl.when(step == NY - 1)
    def _():
        count, rows, width = out.shape
        width_rows = width // count
        scaled = exact(total[...], factor[...], ((0,), (0,)))
        inner = exact(col_panel[...], scaled, ((0,), (0,)))
        out[:, : rows - width_rows, :] = scaled.reshape(count, rows - width_rows, width)
        out[:, rows - width_rows :, :] = inner.reshape(count, width_rows, width)


def product(y, matrix, factor, col_panel, panels, count):
    rows, cols = matrix.shape
    block, width = panels[0].shape
    out_shape = (count, (cols + width) // count, width)

    def moving(s, y_ref):
        return (lax.rem(y_ref[0] + (NY - s), NY), 0)

    def fixed(s, y_ref):
        return (0, 0)

    return pl.pallas_call(
        product_kernel,
        out_shape=jax.ShapeDtypeStruct(out_shape, jnp.float32),
        grid_spec=pltpu.PrefetchScalarGridSpec(
            num_scalar_prefetch=1,
            grid=(NY,),
            in_specs=[
                pl.BlockSpec((block, cols), moving),
                pl.BlockSpec((width, width), fixed),
                pl.BlockSpec((cols, width), fixed),
            ]
            + [pl.BlockSpec((block, width), fixed)] * NY,
            out_specs=pl.BlockSpec(out_shape, lambda s, y_ref: (0, 0, 0)),
            scratch_shapes=[pltpu.VMEM((width, cols), jnp.float32)],
        ),
        cost_estimate=FREE,
        compiler_params=PARAMS,
    )(y, matrix, factor, col_panel, *panels)


def middle_kernel(place, factor, panel, home, col_panel, col_scaled, *refs):
    mine, other = refs[:NX], refs[NX]
    left, correction, small = refs[NX + 1 :]
    assemble(place, mine, other, small)
    width = factor.shape[0]
    kernel = 0.5 * exact(factor[...], small[...].reshape(width, width), ((0,), (0,)))
    correction[...] = home[...] - exact(panel[...], kernel, ((1,), (0,)))
    both = kernel + kernel.T
    left[...] = col_scaled[...] - exact(col_panel[...], both, ((1,), (0,)))


def middle(place, factor, panel, home, col_panel, col_scaled, mine, other):
    shapes = [col_scaled.shape, home.shape]
    return pl.pallas_call(
        middle_kernel,
        out_shape=[jax.ShapeDtypeStruct(shape, jnp.float32) for shape in shapes],
        in_specs=[SCALARS] + [WHOLE] * (5 + NX + 1),
        out_specs=[WHOLE] * 2,
        scratch_shapes=[pltpu.VMEM((NX * CORES,) + mine[0].shape, jnp.float32)],
        cost_estimate=FREE,
        compiler_params=PARAMS,
    )(place, factor, panel, home, col_panel, col_scaled, *mine, other)


def update_kernel(y_ref, matrix, right, *refs):
    parts = refs[:NY]
    out, right_high, right_low = refs[NY:]
    step = pl.program_id(0)

    @pl.when(step == 0)
    def _():
        right_high[...], right_low[...] = halves(right[...])

    for k in range(NY):

        @pl.when(step == k)
        def _():
            pair = right_high[...], right_low[...]
            out[...] = matrix[...] - three_pass(halves(parts[k][...]), pair, ((1,), (1,)))


def update(y, matrix, parts, right, in_place):
    rows, cols = matrix.shape
    block, width = parts[0].shape

    def moving(s, y_ref):
        return (lax.rem(y_ref[0] + (NY - s), NY), 0)

    def fixed(s, y_ref):
        return (0, 0)

    return pl.pallas_call(
        update_kernel,
        out_shape=jax.ShapeDtypeStruct((rows, cols), jnp.float32),
        grid_spec=pltpu.PrefetchScalarGridSpec(
            num_scalar_prefetch=1,
            grid=(NY,),
            in_specs=[pl.BlockSpec((block, cols), moving), pl.BlockSpec((cols, width), fixed)]
            + [pl.BlockSpec((block, width), fixed)] * NY,
            out_specs=pl.BlockSpec((block, cols), moving),
            scratch_shapes=[pltpu.VMEM((cols, width), jnp.bfloat16)] * 2,
        ),
        input_output_aliases={1: 0} if in_place else {},
        cost_estimate=FREE,
        compiler_params=PARAMS,
    )(y, matrix, right, *parts)


def per_device(matrix, panel, factor):
    nrows, ncols = lax.axis_size("row"), lax.axis_size("col")
    rows, width = panel.shape
    block = NZ * rows
    row = lax.axis_index("row")
    y = (lax.axis_index("col") // NZ).reshape(1)
    place = jnp.stack([row // CORES, row % CORES])
    total = nrows * ncols
    to_column = [(g, g % nrows * ncols + g // nrows) for g in range(total)]
    to_home = [(b, a) for a, b in to_column]

    mine = x_blocks(lax.ppermute(panel, ("row", "col"), to_column))
    own_panel = spread(panel, Z_GROUPS).reshape(block, width)
    panels = y_blocks(own_panel)
    col_panel = row_blocks(place, mine, other_core(mine)).reshape(nrows * rows, width)

    parts = product(y, matrix, factor, col_panel, panels, nrows)
    parts = jnp.sum(lax.all_to_all(parts, "row", 0, 0), axis=0)
    chunk, inner = parts[:rows], parts[rows:]

    home = lax.ppermute(chunk, ("row", "col"), to_home)
    inner = sum(y_blocks(inner))
    own_scaled = spread(after(home, inner), Z_GROUPS).reshape(block, width)
    mine = x_blocks(after(chunk, home))
    inner = z_sum(inner)
    own_scaled = after(own_scaled, inner)
    col_scaled = row_blocks(place, mine, other_core(mine)).reshape(nrows * rows, width)
    scaleds = y_blocks(own_scaled)

    mine = x_blocks(after(inner, own_scaled))
    left, correction = middle(
        place, factor, panel, home, col_panel, col_scaled, mine, other_core(mine)
    )
    updated = update(y, matrix, panels, left, False)
    return update(y, updated, scaleds, col_panel, True), correction


def solution(mesh):
    in_specs = (P("row", "col"), P(("row", "col"), None), P())
    out_specs = (P("row", "col"), P(("row", "col"), None))
    return jax.shard_map(
        per_device, mesh=mesh, in_specs=in_specs, out_specs=out_specs, check_vma=False
    )
```

```python
import jax
import jax.numpy as jnp
from jax import lax
from jax.experimental import pallas as pl
from jax.experimental.pallas import tpu as pltpu
from jax.sharding import PartitionSpec as P

NX, NY, NZ, CORES = 4, 4, 8, 2
Z_GROUPS = [[y * NZ + z for z in range(NZ)] for y in range(NY)]
WHOLE = pl.BlockSpec(memory_space=pltpu.VMEM)
SCALARS = pl.BlockSpec(memory_space=pltpu.SMEM)
TILE = 256
FREE = pl.CostEstimate(flops=1, bytes_accessed=1, transcendentals=0)
PARAMS = pltpu.CompilerParams(vmem_limit_bytes=28 << 20)
LARGE = pltpu.CompilerParams(vmem_limit_bytes=48 << 20)


def after(value, *others):
    return lax.optimization_barrier((value,) + others)[0]


def exact(left, right, contract):
    return lax.dot_general(
        left,
        right,
        (contract, ((), ())),
        precision=lax.Precision.HIGHEST,
        preferred_element_type=jnp.float32,
    )


def halves(value):
    high = value.astype(jnp.bfloat16)
    return high, (value - high.astype(jnp.float32)).astype(jnp.bfloat16)


def three_terms(value, axis, right):
    high, low = halves(value)
    return jnp.concatenate([low, high, high] if right else [high, low, high], axis=axis)


def contracted(left, right, axis):
    contract = (((axis,), (axis,)), ((), ()))
    return lax.dot_general(left, right, contract, preferred_element_type=jnp.float32)


def spread(value, groups):
    copies = jnp.broadcast_to(value, (len(groups[0]),) + value.shape)
    return lax.all_to_all(copies, "col", 0, 0, axis_index_groups=groups)


def y_shift(value, step):
    perm = [(y * NZ + z, (y + step) % NY * NZ + z) for y in range(NY) for z in range(NZ)]
    return lax.ppermute(value, "col", perm)


def y_sum(value):
    return value + y_shift(value, 1) + y_shift(value, 2) + y_shift(value, 3)


def y_halves(value):
    first, second = value[:TILE], value[TILE:]
    up_first, down_second = y_shift(first, 1), y_shift(second, -1)
    up_second, down_first = y_shift(second, 1), y_shift(first, -1)
    far_first, far_second = y_shift(up_first, 1), y_shift(down_second, -1)
    return [first, second, up_first, up_second, far_first, far_second, down_first, down_second]


def z_step(value, bit):
    perm = [(y * NZ + z, y * NZ + (z ^ bit)) for y in range(NY) for z in range(NZ)]
    return value + lax.ppermute(value, "col", perm)


def x_blocks(value):
    size = NX * CORES

    def shifted(step):
        perm = [(i, (i - CORES * step) % size) for i in range(size)]
        return lax.ppermute(value, "row", perm)

    return [value] + [shifted(step) for step in range(1, NX)]


def other_core(values):
    perm = [(i, i ^ 1) for i in range(NX * CORES)]
    return lax.ppermute(jnp.stack(values), "row", perm)


def assemble(place, mine, other, out):
    for k in range(NX):
        slot = lax.rem(place[0] + k, NX) * CORES
        out[slot + place[1]] = mine[k][...]
        out[slot + 1 - place[1]] = other[k]


def assemble_kernel(place, *refs):
    assemble(place, refs[:NX], refs[NX], refs[NX + 1])


def row_blocks(place, mine, other):
    shape = (NX * CORES,) + mine[0].shape
    return pl.pallas_call(
        assemble_kernel,
        out_shape=jax.ShapeDtypeStruct(shape, mine[0].dtype),
        in_specs=[SCALARS] + [WHOLE] * (NX + 1),
        out_specs=WHOLE,
        cost_estimate=FREE,
        compiler_params=PARAMS,
    )(place, *mine, other)


def tile_of(step, y_ref):
    return lax.rem(y_ref[0] + (NY - step // 2), NY) * 2 + step % 2


def product_kernel(y_ref, matrix, factor, col_panel, *refs):
    parts, out, total = refs[: 2 * NY], refs[2 * NY], refs[2 * NY + 1]
    step = pl.program_id(0)
    for k in range(2 * NY):

        @pl.when(step == k)
        def _():
            left = three_terms(parts[k][...], 0, False)
            piece = contracted(left, three_terms(matrix[...], 0, True), 0)
            if k == 0:
                total[...] = piece
            else:
                total[...] += piece

    @pl.when(step == 2 * NY - 1)
    def _():
        count, rows, width = out.shape
        width_rows = width // count
        scaled = exact(total[...], factor[...], ((0,), (0,)))
        inner = exact(col_panel[...], scaled, ((0,), (0,)))
        out[:, : rows - width_rows, :] = scaled.reshape(count, rows - width_rows, width)
        out[:, rows - width_rows :, :] = inner.reshape(count, width_rows, width)


def product(y, matrix, factor, col_panel, parts, count):
    cols, width = matrix.shape[1], factor.shape[0]
    out_shape = (count, (cols + width) // count, width)

    def moving(step, y_ref):
        return (tile_of(step, y_ref), 0)

    def fixed(step, y_ref):
        return (0, 0)

    return pl.pallas_call(
        product_kernel,
        out_shape=jax.ShapeDtypeStruct(out_shape, jnp.float32),
        grid_spec=pltpu.PrefetchScalarGridSpec(
            num_scalar_prefetch=1,
            grid=(2 * NY,),
            in_specs=[
                pl.BlockSpec((TILE, cols), moving),
                pl.BlockSpec((width, width), fixed),
                pl.BlockSpec((cols, width), fixed),
            ]
            + [pl.BlockSpec((TILE, width), fixed)] * (2 * NY),
            out_specs=pl.BlockSpec(out_shape, lambda step, y_ref: (0, 0, 0)),
            scratch_shapes=[pltpu.VMEM((width, cols), jnp.float32)],
        ),
        cost_estimate=FREE,
        compiler_params=LARGE,
    )(y, matrix, factor, col_panel, *parts)


def middle_kernel(place, factor, panel, home, col_panel, col_scaled, *refs):
    mine, other = refs[:NX], refs[NX]
    left, correction, small = refs[NX + 1 :]
    assemble(place, mine, other, small)
    width = factor.shape[0]
    kernel = 0.5 * exact(factor[...], small[...].reshape(width, width), ((0,), (0,)))
    correction[...] = home[...] - exact(panel[...], kernel, ((1,), (0,)))
    both = kernel + kernel.T
    left[...] = col_scaled[...] - exact(col_panel[...], both, ((1,), (0,)))


def middle(place, factor, panel, home, col_panel, col_scaled, mine, other):
    shapes = [col_scaled.shape, home.shape]
    operands = [factor, panel, home, col_panel, col_scaled, *mine, other]

    def whole(shape):
        return pl.BlockSpec(shape, lambda step: (0,) * len(shape))

    return pl.pallas_call(
        middle_kernel,
        out_shape=[jax.ShapeDtypeStruct(shape, jnp.float32) for shape in shapes],
        grid=(1,),
        in_specs=[SCALARS] + [whole(operand.shape) for operand in operands],
        out_specs=[whole(shape) for shape in shapes],
        scratch_shapes=[pltpu.VMEM((NX * CORES,) + mine[0].shape, jnp.float32)],
        cost_estimate=FREE,
        compiler_params=PARAMS,
    )(place, *operands)


def update_kernel(y_ref, matrix, right, *refs):
    parts, (out, terms) = refs[:-2], refs[-2:]
    step = pl.program_id(0)

    @pl.when(step == 0)
    def _():
        terms[...] = three_terms(right[...], 1, True)

    for k in range(len(parts)):

        @pl.when(step == k)
        def _():
            left = three_terms(parts[k][...], 1, False)
            out[...] = matrix[...] - contracted(left, terms[...], 1)


def update(y, matrix, parts, right, first, in_place):
    rows, cols = matrix.shape
    width = right.shape[1]

    def moving(step, y_ref):
        return (tile_of(step + first, y_ref), 0)

    def fixed(step, y_ref):
        return (0, 0)

    return pl.pallas_call(
        update_kernel,
        out_shape=jax.ShapeDtypeStruct((rows, cols), jnp.float32),
        grid_spec=pltpu.PrefetchScalarGridSpec(
            num_scalar_prefetch=1,
            grid=(len(parts),),
            in_specs=[pl.BlockSpec((TILE, cols), moving), pl.BlockSpec((cols, width), fixed)]
            + [pl.BlockSpec((TILE, width), fixed)] * len(parts),
            out_specs=pl.BlockSpec((TILE, cols), moving),
            scratch_shapes=[pltpu.VMEM((cols, 3 * width), jnp.bfloat16)],
        ),
        input_output_aliases={1: 0} if in_place else {},
        cost_estimate=FREE,
        compiler_params=LARGE,
    )(y, matrix, right, *parts)


def per_device(matrix, panel, factor):
    nrows, ncols = lax.axis_size("row"), lax.axis_size("col")
    rows, width = panel.shape
    block = NZ * rows
    row = lax.axis_index("row")
    y = (lax.axis_index("col") // NZ).reshape(1)
    place = jnp.stack([row // CORES, row % CORES])
    total = nrows * ncols
    to_column = [(g, g % nrows * ncols + g // nrows) for g in range(total)]
    to_home = [(b, a) for a, b in to_column]

    moved = lax.ppermute(panel, ("row", "col"), to_column)
    own_panel = after(spread(panel, Z_GROUPS).reshape(block, width), moved)
    panels = y_halves(own_panel)
    mine = x_blocks(after(moved, own_panel))
    col_panel = row_blocks(place, mine, other_core(mine)).reshape(nrows * rows, width)

    parts = product(y, matrix, factor, col_panel, panels, nrows)
    parts = jnp.sum(lax.all_to_all(parts, "row", 0, 0), axis=0)
    chunk, inner = parts[:rows], parts[rows:]

    home = lax.ppermute(chunk, ("row", "col"), to_home)
    inner = z_step(z_step(inner, 1), 2)
    own_scaled = spread(after(home, inner), Z_GROUPS).reshape(block, width)
    inner = y_sum(z_step(inner, 4))
    mine = x_blocks(after(chunk, home))
    own_scaled = after(own_scaled, inner, *mine)
    scaleds = y_halves(own_scaled)
    col_scaled = row_blocks(place, mine, other_core(mine)).reshape(nrows * rows, width)

    mine = x_blocks(after(inner, own_scaled))
    left, correction = middle(
        place, factor, panel, home, col_panel, col_scaled, mine, other_core(mine)
    )
    updated = update(y, matrix, panels, left, 0, False)
    updated = update(y, updated, scaleds[:2], col_panel, 0, True)
    return update(y, updated, scaleds[2:], col_panel, 2, True), correction


def solution(mesh):
    in_specs = (P("row", "col"), P(("row", "col"), None), P())
    out_specs = (P("row", "col"), P(("row", "col"), None))
    return jax.shard_map(
        per_device, mesh=mesh, in_specs=in_specs, out_specs=out_specs, check_vma=False
    )
```

```python
import jax
import jax.numpy as jnp
from jax import lax
from jax.experimental import pallas as pl
from jax.experimental.pallas import tpu as pltpu
from jax.sharding import PartitionSpec as P

NX, NY, NZ, CORES = 4, 4, 8, 2
Z_GROUPS = [[y * NZ + z for z in range(NZ)] for y in range(NY)]
WHOLE = pl.BlockSpec(memory_space=pltpu.VMEM)
SCALARS = pl.BlockSpec(memory_space=pltpu.SMEM)
FREE = pl.CostEstimate(flops=1, bytes_accessed=1, transcendentals=0)
PARAMS = pltpu.CompilerParams(vmem_limit_bytes=20 << 20)


def after(value, *others):
    return lax.optimization_barrier((value,) + others)[0]


def exact(left, right, contract):
    return lax.dot_general(
        left,
        right,
        (contract, ((), ())),
        precision=lax.Precision.HIGHEST,
        preferred_element_type=jnp.float32,
    )


def halves(value):
    high = value.astype(jnp.bfloat16)
    return high, (value - high.astype(jnp.float32)).astype(jnp.bfloat16)


def three_pass(left, right, contract):
    def one(a, b):
        return lax.dot_general(a, b, (contract, ((), ())), preferred_element_type=jnp.float32)

    return one(left[0], right[1]) + one(left[1], right[0]) + one(left[0], right[0])


def spread(value, groups):
    copies = jnp.broadcast_to(value, (len(groups[0]),) + value.shape)
    return lax.all_to_all(copies, "col", 0, 0, axis_index_groups=groups)


def y_blocks(value):
    def shifted(step):
        perm = [(y * NZ + z, (y + step) % NY * NZ + z) for y in range(NY) for z in range(NZ)]
        return lax.ppermute(value, "col", perm)

    return [value] + [shifted(step) for step in range(1, NY)]


def y_sum(value):
    for bit in (1, 2):
        perm = [(y * NZ + z, (y ^ bit) * NZ + z) for y in range(NY) for z in range(NZ)]
        value += lax.ppermute(value, "col", perm)
    return value


def x_blocks(value):
    size = NX * CORES

    def shifted(step):
        perm = [(i, (i - CORES * step) % size) for i in range(size)]
        return lax.ppermute(value, "row", perm)

    return [value] + [shifted(step) for step in range(1, NX)]


def other_core(values):
    perm = [(i, i ^ 1) for i in range(NX * CORES)]
    return lax.ppermute(jnp.stack(values), "row", perm)


def assemble(place, mine, other, out):
    for k in range(NX):
        slot = lax.rem(place[0] + k, NX) * CORES
        out[slot + place[1]] = mine[k][...]
        out[slot + 1 - place[1]] = other[k]


def assemble_kernel(place, *refs):
    assemble(place, refs[:NX], refs[NX], refs[NX + 1])


def row_blocks(place, mine, other):
    shape = (NX * CORES,) + mine[0].shape
    return pl.pallas_call(
        assemble_kernel,
        out_shape=jax.ShapeDtypeStruct(shape, mine[0].dtype),
        in_specs=[SCALARS] + [WHOLE] * (NX + 1),
        out_specs=WHOLE,
        cost_estimate=FREE,
        compiler_params=PARAMS,
    )(place, *mine, other)


def local(kernel, shapes, operands, scratch=(), scalars=1):
    single = not isinstance(shapes, list)
    shapes = [shapes] if single else shapes
    results = pl.pallas_call(
        kernel,
        out_shape=[jax.ShapeDtypeStruct(shape, jnp.float32) for shape in shapes],
        in_specs=[SCALARS] * scalars + [WHOLE] * (len(operands) - scalars),
        out_specs=[WHOLE] * len(shapes),
        scratch_shapes=scratch,
        cost_estimate=FREE,
        compiler_params=PARAMS,
    )(*operands)
    return results[0] if single else results


def stage_kernel(matrix, out):
    pltpu.sync_copy(matrix, out)


def stage(matrix):
    return pl.pallas_call(
        stage_kernel,
        out_shape=jax.ShapeDtypeStruct(matrix.shape, matrix.dtype),
        in_specs=[pl.BlockSpec(memory_space=pl.ANY)],
        out_specs=WHOLE,
        cost_estimate=FREE,
        compiler_params=PARAMS,
    )(matrix)


def rows_of(y_ref, step, size):
    return pl.ds(pl.multiple_of(lax.rem(y_ref[0] + (NY - step), NY) * size, size), size)


def product_kernel(y_ref, matrix, factor, col_panel, *refs):
    panels, out, total = refs[:NY], refs[NY], refs[NY + 1]
    for k in range(NY):
        block = matrix[rows_of(y_ref, k, panels[k].shape[0]), :]
        piece = three_pass(halves(panels[k][...]), halves(block), ((0,), (0,)))
        if k == 0:
            total[...] = piece
        else:
            total[...] += piece
    count, rows, width = out.shape
    depth = width // count
    scaled = exact(total[...], factor[...], ((0,), (0,)))
    inner = exact(col_panel[...], scaled, ((0,), (0,)))
    out[:, : rows - depth, :] = scaled.reshape(count, rows - depth, width)
    out[:, rows - depth :, :] = inner.reshape(count, depth, width)


def reduce_kernel(parts, chunk, inner):
    total = parts[0]
    for k in range(1, parts.shape[0]):
        total += parts[k]
    chunk[...] = total[: chunk.shape[0]]
    inner[...] = total[chunk.shape[0] :]


def split_kernel(parts, block, inner):
    rows = block.shape[1]
    block[...] = parts[:, :rows, :]
    total = parts[0, rows:, :]
    for k in range(1, parts.shape[0]):
        total += parts[k, rows:, :]
    inner[...] = total


def middle_kernel(place, factor, panel, home, col_panel, *refs):
    blocks, (left, correction, scaled, small) = refs[:-4], refs[-4:]
    half = NX + 1
    assemble(place, blocks[:NX], blocks[NX], scaled)
    assemble(place, blocks[half : half + NX], blocks[half + NX], small)
    width = panel.shape[1]
    kernel = 0.5 * exact(factor[...], small[...].reshape(width, width), ((0,), (0,)))
    correction[...] = home[...] - exact(panel[...], kernel, ((1,), (0,)))
    wanted = exact(col_panel[...], kernel + kernel.T, ((1,), (0,)))
    left[...] = scaled[...].reshape(left.shape) - wanted


def first_update_kernel(y_ref, matrix, left, col_panel, own_scaled, *refs):
    panels, out = refs[:NY], refs[NY]
    right = halves(left[...])
    for k in range(NY):
        rows = rows_of(y_ref, k, panels[k].shape[0])
        value = matrix[rows, :] - three_pass(halves(panels[k][...]), right, ((1,), (1,)))
        if k == 0:
            pair = halves(own_scaled[...]), halves(col_panel[...])
            value -= three_pass(*pair, ((1,), (1,)))
        out[rows, :] = value


def last_update_kernel(y_ref, matrix, right, *refs):
    parts = refs[: NY - 1]
    out, right_high, right_low = refs[NY - 1 :]
    step = pl.program_id(0)

    @pl.when(step == 0)
    def _():
        right_high[...], right_low[...] = halves(right[...])
        out[...] = matrix[...]

    for k in range(1, NY):

        @pl.when(step == k)
        def _():
            pair = right_high[...], right_low[...]
            out[...] = matrix[...] - three_pass(halves(parts[k - 1][...]), pair, ((1,), (1,)))


def last_update(y, matrix, parts, right):
    rows, cols = matrix.shape
    block, width = parts[0].shape

    def moving(s, y_ref):
        return (lax.rem(y_ref[0] + (NY - s), NY), 0)

    def fixed(s, y_ref):
        return (0, 0)

    return pl.pallas_call(
        last_update_kernel,
        out_shape=jax.ShapeDtypeStruct((rows, cols), jnp.float32),
        grid_spec=pltpu.PrefetchScalarGridSpec(
            num_scalar_prefetch=1,
            grid=(NY,),
            in_specs=[pl.BlockSpec((block, cols), moving), pl.BlockSpec((cols, width), fixed)]
            + [pl.BlockSpec((block, width), fixed)] * (NY - 1),
            out_specs=pl.BlockSpec((block, cols), moving),
            scratch_shapes=[pltpu.VMEM((cols, width), jnp.bfloat16)] * 2,
        ),
        cost_estimate=FREE,
        compiler_params=PARAMS,
    )(y, matrix, right, *parts)


def per_device(matrix, panel, factor):
    nrows, ncols = lax.axis_size("row"), lax.axis_size("col")
    rows, width = panel.shape
    block = NZ * rows
    row = lax.axis_index("row")
    y = (lax.axis_index("col") // NZ).reshape(1)
    place = jnp.stack([row // CORES, row % CORES])
    total = nrows * ncols
    to_column = [(g, g % nrows * ncols + g // nrows) for g in range(total)]
    to_home = [(b, a) for a, b in to_column]

    moved = lax.ppermute(panel, ("row", "col"), to_column)
    mine = x_blocks(moved)
    panels = y_blocks(spread(panel, Z_GROUPS).reshape(block, width))
    col_panel = row_blocks(place, mine, other_core(mine)).reshape(nrows * rows, width)
    staged = stage(after(matrix, moved))

    depth = width // nrows
    parts = local(
        product_kernel,
        (nrows, rows + depth, width),
        (y, staged, factor, col_panel, *panels),
        [pltpu.VMEM((width, nrows * rows), jnp.float32)],
    )
    parts = lax.all_to_all(parts, "row", 0, 0)
    pair = [(rows, width), (depth, width)]
    chunk, inner = local(reduce_kernel, pair, (parts,), scalars=0)

    home = lax.ppermute(chunk, ("row", "col"), to_home)
    parts = spread(jnp.concatenate([home, y_sum(inner)]), Z_GROUPS)
    scaled = x_blocks(after(chunk, home))
    scaled += [other_core(scaled)]
    parts = after(parts, *scaled)
    pair = [(NZ, rows, width), (depth, width)]
    own_scaled, inner = local(split_kernel, pair, (parts,), scalars=0)
    scaleds = y_blocks(own_scaled.reshape(block, width))

    small = x_blocks(after(inner, own_scaled))
    small += [other_core(small)]
    left, correction = local(
        middle_kernel,
        [col_panel.shape, home.shape],
        (place, factor, panel, home, col_panel, *scaled, *small),
        [pltpu.VMEM((nrows, size, width), jnp.float32) for size in (rows, depth)],
    )
    updated = local(
        first_update_kernel, matrix.shape, (y, staged, left, col_panel, scaleds[0], *panels)
    )
    return last_update(y, updated, scaleds[1:], col_panel), correction


def solution(mesh):
    in_specs = (P("row", "col"), P(("row", "col"), None), P())
    out_specs = (P("row", "col"), P(("row", "col"), None))
    return jax.shard_map(
        per_device, mesh=mesh, in_specs=in_specs, out_specs=out_specs, check_vma=False
    )
```

```python
import jax
import jax.numpy as jnp
from jax import lax
from jax.experimental import pallas as pl
from jax.experimental.pallas import tpu as pltpu
from jax.sharding import PartitionSpec as P

NX, NY, NZ, CORES = 4, 4, 8, 2
Z_GROUPS = [[y * NZ + z for z in range(NZ)] for y in range(NY)]
WHOLE = pl.BlockSpec(memory_space=pltpu.VMEM)
SCALARS = pl.BlockSpec(memory_space=pltpu.SMEM)
MIDDLE = 44
FREE = pl.CostEstimate(flops=1, bytes_accessed=1, transcendentals=0)
PARAMS = pltpu.CompilerParams(vmem_limit_bytes=44 << 20)


def after(value, *others):
    return lax.optimization_barrier((value,) + others)[0]


def exact(left, right, contract):
    return lax.dot_general(
        left,
        right,
        (contract, ((), ())),
        precision=lax.Precision.HIGHEST,
        preferred_element_type=jnp.float32,
    )


def halves(value):
    high = value.astype(jnp.bfloat16)
    return high, (value - high.astype(jnp.float32)).astype(jnp.bfloat16)


def three_pass(left, right, contract):
    def one(a, b):
        return lax.dot_general(a, b, (contract, ((), ())), preferred_element_type=jnp.float32)

    return one(left[0], right[1]) + one(left[1], right[0]) + one(left[0], right[0])


def spread(value, groups):
    copies = jnp.broadcast_to(value, (len(groups[0]),) + value.shape)
    return lax.all_to_all(copies, "col", 0, 0, axis_index_groups=groups)


def y_blocks(value):
    def shifted(step):
        perm = [(y * NZ + z, (y + step) % NY * NZ + z) for y in range(NY) for z in range(NZ)]
        return lax.ppermute(value, "col", perm)

    return [value] + [shifted(step) for step in range(1, NY)]


def z_sum(value):
    def partner(value, bits):
        perm = [(y * NZ + z, y * NZ + (z ^ bits)) for y in range(NY) for z in range(NZ)]
        return lax.ppermute(value, "col", perm)

    value = sum([partner(value, bits) for bits in (1, 2, 3)], value)
    return value + partner(value, 4)


def x_blocks(value):
    size = NX * CORES

    def shifted(step):
        perm = [(i, (i - CORES * step) % size) for i in range(size)]
        return lax.ppermute(value, "row", perm)

    return [value] + [shifted(step) for step in range(1, NX)]


def other_core(values):
    perm = [(i, i ^ 1) for i in range(NX * CORES)]
    return lax.ppermute(jnp.stack(values), "row", perm)


def assemble(place, mine, other, out):
    for k in range(NX):
        slot = lax.rem(place[0] + k, NX) * CORES
        out[slot + place[1]] = mine[k][...]
        out[slot + 1 - place[1]] = other[k]


def assemble_kernel(place, *refs):
    assemble(place, refs[:NX], refs[NX], refs[NX + 1])


def row_blocks(place, mine, other):
    shape = (NX * CORES,) + mine[0].shape
    return pl.pallas_call(
        assemble_kernel,
        out_shape=jax.ShapeDtypeStruct(shape, mine[0].dtype),
        in_specs=[SCALARS] + [WHOLE] * (NX + 1),
        out_specs=WHOLE,
        cost_estimate=FREE,
        compiler_params=PARAMS,
    )(place, *mine, other)


def local(kernel, shapes, operands, scratch=(), scalars=1):
    single = not isinstance(shapes, list)
    shapes = [shapes] if single else shapes
    results = pl.pallas_call(
        kernel,
        out_shape=[jax.ShapeDtypeStruct(shape, jnp.float32) for shape in shapes],
        in_specs=[SCALARS] * scalars + [WHOLE] * (len(operands) - scalars),
        out_specs=[WHOLE] * len(shapes),
        scratch_shapes=scratch,
        cost_estimate=FREE,
        compiler_params=PARAMS,
    )(*operands)
    return results[0] if single else results


def stage_kernel(matrix, out):
    pltpu.sync_copy(matrix, out)


def stage(matrix):
    return pl.pallas_call(
        stage_kernel,
        out_shape=jax.ShapeDtypeStruct(matrix.shape, matrix.dtype),
        in_specs=[pl.BlockSpec(memory_space=pl.ANY)],
        out_specs=WHOLE,
        cost_estimate=FREE,
        compiler_params=PARAMS,
    )(matrix)


def rows_of(y_ref, step, size):
    return pl.ds(pl.multiple_of(lax.rem(y_ref[0] + (NY - step), NY) * size, size), size)


def product_kernel(y_ref, matrix, factor, col_panel, *refs):
    panels, out, total = refs[:NY], refs[NY], refs[NY + 1]
    for k in range(NY):
        block = matrix[rows_of(y_ref, k, panels[k].shape[0]), :]
        piece = three_pass(halves(panels[k][...]), halves(block), ((0,), (0,)))
        if k == 0:
            total[...] = piece
        else:
            total[...] += piece
    count, rows, width = out.shape
    depth = width // count
    scaled = exact(total[...], factor[...], ((0,), (0,)))
    inner = exact(col_panel[...], scaled, ((0,), (0,)))
    out[:, : rows - depth, :] = scaled.reshape(count, rows - depth, width)
    out[:, rows - depth :, :] = inner.reshape(count, depth, width)


def reduce_kernel(parts, chunk, inner):
    total = parts[0]
    for k in range(1, parts.shape[0]):
        total += parts[k]
    chunk[...] = total[: chunk.shape[0]]
    inner[...] = total[chunk.shape[0] :]


def middle_kernel(place, factor, panel, home, col_panel, *refs):
    blocks, (left, correction, scaled, small) = refs[:-4], refs[-4:]
    half = NX + 1
    assemble(place, blocks[:NX], blocks[NX], scaled)
    assemble(place, blocks[half : half + NX], blocks[half + NX], small)
    width = panel.shape[1]
    kernel = 0.5 * exact(factor[...], small[...].reshape(width, width), ((0,), (0,)))
    correction[...] = home[...] - exact(panel[...], kernel, ((1,), (0,)))
    wanted = exact(col_panel[...], kernel + kernel.T, ((1,), (0,)))
    left[...] = scaled[...].reshape(left.shape) - wanted


def middle(place, operands, shapes, scratch):
    def whole(shape):
        return pl.BlockSpec(shape, lambda step: (0,) * len(shape))

    return pl.pallas_call(
        middle_kernel,
        out_shape=[jax.ShapeDtypeStruct(shape, jnp.float32) for shape in shapes],
        grid=(1,),
        in_specs=[SCALARS] + [whole(operand.shape) for operand in operands],
        out_specs=[whole(shape) for shape in shapes],
        scratch_shapes=scratch,
        cost_estimate=FREE,
        compiler_params=pltpu.CompilerParams(vmem_limit_bytes=MIDDLE << 20),
    )(place, *operands)


def first_update_kernel(y_ref, matrix, left, col_panel, own_scaled, *refs):
    panels, out = refs[:NY], refs[NY]
    right = halves(left[...])
    for k in range(NY):
        rows = rows_of(y_ref, k, panels[k].shape[0])
        value = matrix[rows, :] - three_pass(halves(panels[k][...]), right, ((1,), (1,)))
        if k == 0:
            pair = halves(own_scaled[...]), halves(col_panel[...])
            value -= three_pass(*pair, ((1,), (1,)))
        out[rows, :] = value


def last_update_kernel(y_ref, matrix, right, *refs):
    parts = refs[: NY - 1]
    out, right_high, right_low = refs[NY - 1 :]
    step = pl.program_id(0)

    @pl.when(step == 0)
    def _():
        right_high[...], right_low[...] = halves(right[...])
        out[...] = matrix[...]

    for k in range(1, NY):

        @pl.when(step == k)
        def _():
            pair = right_high[...], right_low[...]
            out[...] = matrix[...] - three_pass(halves(parts[k - 1][...]), pair, ((1,), (1,)))


def last_update(y, matrix, parts, right):
    rows, cols = matrix.shape
    block, width = parts[0].shape

    def moving(s, y_ref):
        return (lax.rem(y_ref[0] + (NY - s), NY), 0)

    def fixed(s, y_ref):
        return (0, 0)

    return pl.pallas_call(
        last_update_kernel,
        out_shape=jax.ShapeDtypeStruct((rows, cols), jnp.float32),
        grid_spec=pltpu.PrefetchScalarGridSpec(
            num_scalar_prefetch=1,
            grid=(NY,),
            in_specs=[pl.BlockSpec((block, cols), moving), pl.BlockSpec((cols, width), fixed)]
            + [pl.BlockSpec((block, width), fixed)] * (NY - 1),
            out_specs=pl.BlockSpec((block, cols), moving),
            scratch_shapes=[pltpu.VMEM((cols, width), jnp.bfloat16)] * 2,
        ),
        cost_estimate=FREE,
        compiler_params=PARAMS,
    )(y, matrix, right, *parts)


def per_device(matrix, panel, factor):
    nrows, ncols = lax.axis_size("row"), lax.axis_size("col")
    rows, width = panel.shape
    block = NZ * rows
    row = lax.axis_index("row")
    y = (lax.axis_index("col") // NZ).reshape(1)
    place = jnp.stack([row // CORES, row % CORES])
    total = nrows * ncols
    to_column = [(g, g % nrows * ncols + g // nrows) for g in range(total)]
    to_home = [(b, a) for a, b in to_column]

    moved = lax.ppermute(panel, ("row", "col"), to_column)
    mine = x_blocks(moved)
    panels = y_blocks(spread(panel, Z_GROUPS).reshape(block, width))
    col_panel = row_blocks(place, mine, other_core(mine)).reshape(nrows * rows, width)
    staged = stage(after(matrix, moved))

    depth = width // nrows
    parts = local(
        product_kernel,
        (nrows, rows + depth, width),
        (y, staged, factor, col_panel, *panels),
        [pltpu.VMEM((width, nrows * rows), jnp.float32)],
    )
    parts = lax.all_to_all(parts, "row", 0, 0)
    pair = [(rows, width), (depth, width)]
    chunk, inner = local(reduce_kernel, pair, (parts,), scalars=0)

    home = lax.ppermute(chunk, ("row", "col"), to_home)
    inner = z_sum(inner)
    own_scaled = spread(after(home, inner), Z_GROUPS).reshape(block, width)
    inner = sum(y_blocks(inner))
    scaled = x_blocks(after(chunk, home))
    own_scaled = after(own_scaled, inner, *scaled)
    scaleds = y_blocks(own_scaled)

    small = x_blocks(after(inner, own_scaled))
    small += [other_core(small)]
    scaled += [other_core(scaled)]
    left, correction = middle(
        place,
        (factor, panel, home, col_panel, *scaled, *small),
        [col_panel.shape, home.shape],
        [pltpu.VMEM((nrows, size, width), jnp.float32) for size in (rows, depth)],
    )
    updated = local(
        first_update_kernel, matrix.shape, (y, staged, left, col_panel, scaleds[0], *panels)
    )
    return last_update(y, updated, scaleds[1:], col_panel), correction


def solution(mesh):
    in_specs = (P("row", "col"), P(("row", "col"), None), P())
    out_specs = (P("row", "col"), P(("row", "col"), None))
    return jax.shard_map(
        per_device, mesh=mesh, in_specs=in_specs, out_specs=out_specs, check_vma=False
    )
```

```python
import jax
import jax.numpy as jnp
from jax import lax
from jax.experimental import pallas as pl
from jax.experimental.pallas import tpu as pltpu
from jax.sharding import PartitionSpec as P

NX, NY, NZ, CORES = 4, 4, 8, 2
Z_GROUPS = [[y * NZ + z for z in range(NZ)] for y in range(NY)]
WHOLE = pl.BlockSpec(memory_space=pltpu.VMEM)
SCALARS = pl.BlockSpec(memory_space=pltpu.SMEM)
MIDDLE = 44
FREE = pl.CostEstimate(flops=1, bytes_accessed=1, transcendentals=0)
PARAMS = pltpu.CompilerParams(vmem_limit_bytes=44 << 20)


def after(value, *others):
    return lax.optimization_barrier((value,) + others)[0]


def exact(left, right, contract):
    return lax.dot_general(
        left,
        right,
        (contract, ((), ())),
        precision=lax.Precision.HIGHEST,
        preferred_element_type=jnp.float32,
    )


def halves(value):
    high = value.astype(jnp.bfloat16)
    return high, (value - high.astype(jnp.float32)).astype(jnp.bfloat16)


def three_pass(left, right, contract):
    def one(a, b):
        return lax.dot_general(a, b, (contract, ((), ())), preferred_element_type=jnp.float32)

    return one(left[0], right[1]) + one(left[1], right[0]) + one(left[0], right[0])


def spread(value, groups):
    copies = jnp.broadcast_to(value, (len(groups[0]),) + value.shape)
    return lax.all_to_all(copies, "col", 0, 0, axis_index_groups=groups)


def y_blocks(value):
    def shifted(step):
        perm = [(y * NZ + z, (y + step) % NY * NZ + z) for y in range(NY) for z in range(NZ)]
        return lax.ppermute(value, "col", perm)

    return [value] + [shifted(step) for step in range(1, NY)]


def z_partner(value, bit):
    perm = [(y * NZ + z, y * NZ + (z ^ bit)) for y in range(NY) for z in range(NZ)]
    return lax.ppermute(value, "col", perm)


def z_scatter(value, z):
    for bit in (4, 2, 1):
        half = value.shape[0] // 2
        upper = z // bit % 2
        mine = lax.dynamic_slice_in_dim(value, upper * half, half, 0)
        theirs = lax.dynamic_slice_in_dim(value, (1 - upper) * half, half, 0)
        value = mine + z_partner(theirs, bit)
    return value


def z_gather(value):
    for bit in (1, 2, 4):
        value = jnp.concatenate([value, z_partner(value, bit)])
    return value


def y_sum_step(value, bit):
    perm = [(y * NZ + z, (y ^ bit) * NZ + z) for y in range(NY) for z in range(NZ)]
    return value + lax.ppermute(value, "col", perm)


def row_sum(value):
    for bit in (1, 2, 4):
        perm = [(i, i ^ bit) for i in range(NX * CORES)]
        value += lax.ppermute(value, "row", perm)
    return value


def x_blocks(value):
    size = NX * CORES

    def shifted(step):
        perm = [(i, (i - CORES * step) % size) for i in range(size)]
        return lax.ppermute(value, "row", perm)

    return [value] + [shifted(step) for step in range(1, NX)]


def other_core(values):
    perm = [(i, i ^ 1) for i in range(NX * CORES)]
    return lax.ppermute(jnp.stack(values), "row", perm)


def assemble(place, mine, other, out):
    for k in range(NX):
        slot = lax.rem(place[0] + k, NX) * CORES
        out[slot + place[1]] = mine[k][...]
        out[slot + 1 - place[1]] = other[k]


def assemble_kernel(place, *refs):
    assemble(place, refs[:NX], refs[NX], refs[NX + 1])


def row_blocks(place, mine, other):
    shape = (NX * CORES,) + mine[0].shape
    return pl.pallas_call(
        assemble_kernel,
        out_shape=jax.ShapeDtypeStruct(shape, mine[0].dtype),
        in_specs=[SCALARS] + [WHOLE] * (NX + 1),
        out_specs=WHOLE,
        cost_estimate=FREE,
        compiler_params=PARAMS,
    )(place, *mine, other)


def local(kernel, shapes, operands, scratch=(), scalars=1):
    single = not isinstance(shapes, list)
    shapes = [shapes] if single else shapes
    results = pl.pallas_call(
        kernel,
        out_shape=[jax.ShapeDtypeStruct(shape, jnp.float32) for shape in shapes],
        in_specs=[SCALARS] * scalars + [WHOLE] * (len(operands) - scalars),
        out_specs=[WHOLE] * len(shapes),
        scratch_shapes=scratch,
        cost_estimate=FREE,
        compiler_params=PARAMS,
    )(*operands)
    return results[0] if single else results


def stage_kernel(matrix, out):
    pltpu.sync_copy(matrix, out)


def stage(matrix):
    return pl.pallas_call(
        stage_kernel,
        out_shape=jax.ShapeDtypeStruct(matrix.shape, matrix.dtype),
        in_specs=[pl.BlockSpec(memory_space=pl.ANY)],
        out_specs=WHOLE,
        cost_estimate=FREE,
        compiler_params=PARAMS,
    )(matrix)


def rows_of(y_ref, step, size):
    return pl.ds(pl.multiple_of(lax.rem(y_ref[0] + (NY - step), NY) * size, size), size)


def product_kernel(y_ref, matrix, factor, col_panel, *refs):
    panels, (out, inner, total) = refs[:NY], refs[NY:]
    for k in range(NY):
        block = matrix[rows_of(y_ref, k, panels[k].shape[0]), :]
        piece = three_pass(halves(panels[k][...]), halves(block), ((0,), (0,)))
        if k == 0:
            total[...] = piece
        else:
            total[...] += piece
    scaled = exact(total[...], factor[...], ((0,), (0,)))
    out[...] = scaled.reshape(out.shape)
    inner[...] = exact(col_panel[...], scaled, ((0,), (0,)))


def reduce_kernel(parts, chunk):
    total = parts[0]
    for k in range(1, parts.shape[0]):
        total += parts[k]
    chunk[...] = total


def middle_kernel(place, factor, panel, home, col_panel, *refs):
    blocks, gathered, (left, correction, scaled, small) = refs[:-5], refs[-5], refs[-4:]
    assemble(place, blocks[:NX], blocks[NX], scaled)
    for k in range(NZ):
        small[place[2 + k]] = gathered[k]
    width = panel.shape[1]
    kernel = 0.5 * exact(factor[...], small[...].reshape(width, width), ((0,), (0,)))
    correction[...] = home[...] - exact(panel[...], kernel, ((1,), (0,)))
    wanted = exact(col_panel[...], kernel + kernel.T, ((1,), (0,)))
    left[...] = scaled[...].reshape(left.shape) - wanted


def middle(place, operands, shapes, scratch):
    def whole(shape):
        return pl.BlockSpec(shape, lambda step: (0,) * len(shape))

    return pl.pallas_call(
        middle_kernel,
        out_shape=[jax.ShapeDtypeStruct(shape, jnp.float32) for shape in shapes],
        grid=(1,),
        in_specs=[SCALARS] + [whole(operand.shape) for operand in operands],
        out_specs=[whole(shape) for shape in shapes],
        scratch_shapes=scratch,
        cost_estimate=FREE,
        compiler_params=pltpu.CompilerParams(vmem_limit_bytes=MIDDLE << 20),
    )(place, *operands)


def first_update_kernel(y_ref, matrix, left, col_panel, own_scaled, *refs):
    panels, out = refs[:NY], refs[NY]
    right = halves(left[...])
    for k in range(NY):
        rows = rows_of(y_ref, k, panels[k].shape[0])
        value = matrix[rows, :] - three_pass(halves(panels[k][...]), right, ((1,), (1,)))
        if k == 0:
            pair = halves(own_scaled[...]), halves(col_panel[...])
            value -= three_pass(*pair, ((1,), (1,)))
        out[rows, :] = value


def last_update_kernel(y_ref, matrix, right, *refs):
    parts = refs[: NY - 1]
    out, right_high, right_low = refs[NY - 1 :]
    step = pl.program_id(0)

    @pl.when(step == 0)
    def _():
        right_high[...], right_low[...] = halves(right[...])
        out[...] = matrix[...]

    for k in range(1, NY):

        @pl.when(step == k)
        def _():
            pair = right_high[...], right_low[...]
            out[...] = matrix[...] - three_pass(halves(parts[k - 1][...]), pair, ((1,), (1,)))


def last_update(y, matrix, parts, right):
    rows, cols = matrix.shape
    block, width = parts[0].shape

    def moving(s, y_ref):
        return (lax.rem(y_ref[0] + (NY - s), NY), 0)

    def fixed(s, y_ref):
        return (0, 0)

    return pl.pallas_call(
        last_update_kernel,
        out_shape=jax.ShapeDtypeStruct((rows, cols), jnp.float32),
        grid_spec=pltpu.PrefetchScalarGridSpec(
            num_scalar_prefetch=1,
            grid=(NY,),
            in_specs=[pl.BlockSpec((block, cols), moving), pl.BlockSpec((cols, width), fixed)]
            + [pl.BlockSpec((block, width), fixed)] * (NY - 1),
            out_specs=pl.BlockSpec((block, cols), moving),
            scratch_shapes=[pltpu.VMEM((cols, width), jnp.bfloat16)] * 2,
        ),
        cost_estimate=FREE,
        compiler_params=PARAMS,
    )(y, matrix, right, *parts)


def per_device(matrix, panel, factor):
    nrows, ncols = lax.axis_size("row"), lax.axis_size("col")
    rows, width = panel.shape
    block = NZ * rows
    row = lax.axis_index("row")
    y = (lax.axis_index("col") // NZ).reshape(1)
    z = lax.axis_index("col") % NZ
    place = jnp.stack([row // CORES, row % CORES] + [z ^ k for k in range(NZ)])
    total = nrows * ncols
    to_column = [(g, g % nrows * ncols + g // nrows) for g in range(total)]
    to_home = [(b, a) for a, b in to_column]

    moved = lax.ppermute(panel, ("row", "col"), to_column)
    mine = x_blocks(moved)
    panels = y_blocks(spread(panel, Z_GROUPS).reshape(block, width))
    col_panel = row_blocks(place, mine, other_core(mine)).reshape(nrows * rows, width)
    staged = stage(after(matrix, moved))

    shares, inner = local(
        product_kernel,
        [(nrows, rows, width), (width, width)],
        (y, staged, factor, col_panel, *panels),
        [pltpu.VMEM((width, nrows * rows), jnp.float32)],
    )
    parts = lax.all_to_all(shares, "row", 0, 0)
    inner = z_scatter(inner, z)
    chunk = local(reduce_kernel, (rows, width), (parts,), scalars=0)

    home = lax.ppermute(chunk, ("row", "col"), to_home)
    inner = y_sum_step(inner, 1)
    own_scaled = spread(after(home, inner), Z_GROUPS).reshape(block, width)
    inner = row_sum(y_sum_step(inner, 2))
    scaled = x_blocks(after(chunk, home))
    own_scaled = after(own_scaled, inner, *scaled)
    scaleds = y_blocks(own_scaled)

    depth = width // NZ
    small = z_gather(after(inner, own_scaled)).reshape(NZ, depth, width)
    scaled += [other_core(scaled)]
    left, correction = middle(
        place,
        (factor, panel, home, col_panel, *scaled, small),
        [col_panel.shape, home.shape],
        [pltpu.VMEM(shape, jnp.float32) for shape in ((nrows, rows, width), small.shape)],
    )
    updated = local(
        first_update_kernel, matrix.shape, (y, staged, left, col_panel, scaleds[0], *panels)
    )
    return last_update(y, updated, scaleds[1:], col_panel), correction


def solution(mesh):
    in_specs = (P("row", "col"), P(("row", "col"), None), P())
    out_specs = (P("row", "col"), P(("row", "col"), None))
    return jax.shard_map(
        per_device, mesh=mesh, in_specs=in_specs, out_specs=out_specs, check_vma=False
    )
```

```python
import jax
import jax.numpy as jnp
from jax import lax
from jax.experimental import pallas as pl
from jax.experimental.pallas import tpu as pltpu
from jax.sharding import PartitionSpec as P

NX, NY, NZ, CORES = 4, 4, 8, 2
Z_GROUPS = [[y * NZ + z for z in range(NZ)] for y in range(NY)]
WHOLE = pl.BlockSpec(memory_space=pltpu.VMEM)
SCALARS = pl.BlockSpec(memory_space=pltpu.SMEM)
MIDDLE = 44
HALF = 256
PIECES = [(0, 0), (1, 0), (2, 0), (2, HALF), (3, 0)]
FREE = pl.CostEstimate(flops=1, bytes_accessed=1, transcendentals=0)
PARAMS = pltpu.CompilerParams(vmem_limit_bytes=44 << 20)


def after(value, *others):
    return lax.optimization_barrier((value,) + others)[0]


def exact(left, right, contract):
    return lax.dot_general(
        left,
        right,
        (contract, ((), ())),
        precision=lax.Precision.HIGHEST,
        preferred_element_type=jnp.float32,
    )


def halves(value):
    high = value.astype(jnp.bfloat16)
    return high, (value - high.astype(jnp.float32)).astype(jnp.bfloat16)


def three_pass(left, right, contract):
    def one(a, b):
        return lax.dot_general(a, b, (contract, ((), ())), preferred_element_type=jnp.float32)

    return one(left[0], right[1]) + one(left[1], right[0]) + one(left[0], right[0])


def spread(value, groups):
    copies = jnp.broadcast_to(value, (len(groups[0]),) + value.shape)
    return lax.all_to_all(copies, "col", 0, 0, axis_index_groups=groups)


def y_shift(value, step):
    perm = [(y * NZ + z, (y + step) % NY * NZ + z) for y in range(NY) for z in range(NZ)]
    return lax.ppermute(value, "col", perm)


def y_blocks(value):
    return [value] + [y_shift(value, step) for step in range(1, NY)]


def y_pieces(value):
    up, down = y_shift(value, 1), y_shift(value, -1)
    return [value, up, y_shift(up[:HALF], 1), y_shift(down[HALF:], -1), down]


def z_sum(value):
    def partner(value, bits):
        perm = [(y * NZ + z, y * NZ + (z ^ bits)) for y in range(NY) for z in range(NZ)]
        return lax.ppermute(value, "col", perm)

    value = sum([partner(value, bits) for bits in (1, 2, 3)], value)
    return value + partner(value, 4)


def x_blocks(value):
    size = NX * CORES

    def shifted(step):
        perm = [(i, (i - CORES * step) % size) for i in range(size)]
        return lax.ppermute(value, "row", perm)

    return [value] + [shifted(step) for step in range(1, NX)]


def other_core(values):
    perm = [(i, i ^ 1) for i in range(NX * CORES)]
    return lax.ppermute(jnp.stack(values), "row", perm)


def assemble(place, mine, other, out):
    for k in range(NX):
        slot = lax.rem(place[0] + k, NX) * CORES
        out[slot + place[1]] = mine[k][...]
        out[slot + 1 - place[1]] = other[k]


def assemble_kernel(place, *refs):
    assemble(place, refs[:NX], refs[NX], refs[NX + 1])


def row_blocks(place, mine, other):
    shape = (NX * CORES,) + mine[0].shape
    return pl.pallas_call(
        assemble_kernel,
        out_shape=jax.ShapeDtypeStruct(shape, mine[0].dtype),
        in_specs=[SCALARS] + [WHOLE] * (NX + 1),
        out_specs=WHOLE,
        cost_estimate=FREE,
        compiler_params=PARAMS,
    )(place, *mine, other)


def local(kernel, shapes, operands, scratch=(), scalars=1):
    single = not isinstance(shapes, list)
    shapes = [shapes] if single else shapes
    results = pl.pallas_call(
        kernel,
        out_shape=[jax.ShapeDtypeStruct(shape, jnp.float32) for shape in shapes],
        in_specs=[SCALARS] * scalars + [WHOLE] * (len(operands) - scalars),
        out_specs=[WHOLE] * len(shapes),
        scratch_shapes=scratch,
        cost_estimate=FREE,
        compiler_params=PARAMS,
    )(*operands)
    return results[0] if single else results


def stage_kernel(matrix, out):
    pltpu.sync_copy(matrix, out)


def stage(matrix):
    return pl.pallas_call(
        stage_kernel,
        out_shape=jax.ShapeDtypeStruct(matrix.shape, matrix.dtype),
        in_specs=[pl.BlockSpec(memory_space=pl.ANY)],
        out_specs=WHOLE,
        cost_estimate=FREE,
        compiler_params=PARAMS,
    )(matrix)


def rows_of(y_ref, k, piece, block):
    below, first = PIECES[k]
    start = lax.rem(y_ref[0] + (NY - below), NY) * block + first
    return pl.ds(pl.multiple_of(start, HALF), piece.shape[0])


def product_kernel(y_ref, matrix, factor, col_panel, *refs):
    pieces, (out, total) = refs[:-2], refs[-2:]
    for k, piece in enumerate(pieces):
        block = matrix[rows_of(y_ref, k, piece, pieces[0].shape[0]), :]
        part = three_pass(halves(piece[...]), halves(block), ((0,), (0,)))
        if k == 0:
            total[...] = part
        else:
            total[...] += part
    count, rows, width = out.shape
    depth = width // count
    scaled = exact(total[...], factor[...], ((0,), (0,)))
    inner = exact(col_panel[...], scaled, ((0,), (0,)))
    out[:, : rows - depth, :] = scaled.reshape(count, rows - depth, width)
    out[:, rows - depth :, :] = inner.reshape(count, depth, width)


def reduce_kernel(parts, chunk, inner):
    total = parts[0]
    for k in range(1, parts.shape[0]):
        total += parts[k]
    chunk[...] = total[: chunk.shape[0]]
    inner[...] = total[chunk.shape[0] :]


def middle_kernel(place, factor, panel, home, col_panel, *refs):
    blocks, (left, correction, scaled, small) = refs[:-4], refs[-4:]
    half = NX + 1
    assemble(place, blocks[:NX], blocks[NX], scaled)
    assemble(place, blocks[half : half + NX], blocks[half + NX], small)
    width = panel.shape[1]
    kernel = 0.5 * exact(factor[...], small[...].reshape(width, width), ((0,), (0,)))
    correction[...] = home[...] - exact(panel[...], kernel, ((1,), (0,)))
    wanted = exact(col_panel[...], kernel + kernel.T, ((1,), (0,)))
    left[...] = scaled[...].reshape(left.shape) - wanted


def middle(place, operands, shapes, scratch):
    def whole(shape):
        return pl.BlockSpec(shape, lambda step: (0,) * len(shape))

    return pl.pallas_call(
        middle_kernel,
        out_shape=[jax.ShapeDtypeStruct(shape, jnp.float32) for shape in shapes],
        grid=(1,),
        in_specs=[SCALARS] + [whole(operand.shape) for operand in operands],
        out_specs=[whole(shape) for shape in shapes],
        scratch_shapes=scratch,
        cost_estimate=FREE,
        compiler_params=pltpu.CompilerParams(vmem_limit_bytes=MIDDLE << 20),
    )(place, *operands)


def first_update_kernel(y_ref, matrix, left, col_panel, own_scaled, *refs):
    pieces, out = refs[:-1], refs[-1]
    right = halves(left[...])
    for k, piece in enumerate(pieces):
        rows = rows_of(y_ref, k, piece, pieces[0].shape[0])
        value = matrix[rows, :] - three_pass(halves(piece[...]), right, ((1,), (1,)))
        if k == 0:
            pair = halves(own_scaled[...]), halves(col_panel[...])
            value -= three_pass(*pair, ((1,), (1,)))
        out[rows, :] = value


def last_update_kernel(y_ref, matrix, right, *refs):
    parts = refs[: NY - 1]
    out, right_high, right_low = refs[NY - 1 :]
    step = pl.program_id(0)

    @pl.when(step == 0)
    def _():
        right_high[...], right_low[...] = halves(right[...])
        out[...] = matrix[...]

    for k in range(1, NY):

        @pl.when(step == k)
        def _():
            pair = right_high[...], right_low[...]
            out[...] = matrix[...] - three_pass(halves(parts[k - 1][...]), pair, ((1,), (1,)))


def last_update(y, matrix, parts, right):
    rows, cols = matrix.shape
    block, width = parts[0].shape

    def moving(s, y_ref):
        return (lax.rem(y_ref[0] + (NY - s), NY), 0)

    def fixed(s, y_ref):
        return (0, 0)

    return pl.pallas_call(
        last_update_kernel,
        out_shape=jax.ShapeDtypeStruct((rows, cols), jnp.float32),
        grid_spec=pltpu.PrefetchScalarGridSpec(
            num_scalar_prefetch=1,
            grid=(NY,),
            in_specs=[pl.BlockSpec((block, cols), moving), pl.BlockSpec((cols, width), fixed)]
            + [pl.BlockSpec((block, width), fixed)] * (NY - 1),
            out_specs=pl.BlockSpec((block, cols), moving),
            scratch_shapes=[pltpu.VMEM((cols, width), jnp.bfloat16)] * 2,
        ),
        cost_estimate=FREE,
        compiler_params=PARAMS,
    )(y, matrix, right, *parts)


def per_device(matrix, panel, factor):
    nrows, ncols = lax.axis_size("row"), lax.axis_size("col")
    rows, width = panel.shape
    block = NZ * rows
    row = lax.axis_index("row")
    y = (lax.axis_index("col") // NZ).reshape(1)
    place = jnp.stack([row // CORES, row % CORES])
    total = nrows * ncols
    to_column = [(g, g % nrows * ncols + g // nrows) for g in range(total)]
    to_home = [(b, a) for a, b in to_column]

    moved = lax.ppermute(panel, ("row", "col"), to_column)
    own_panel = after(spread(panel, Z_GROUPS).reshape(block, width), moved)
    panels = y_pieces(own_panel)
    mine = x_blocks(after(moved, own_panel))
    col_panel = row_blocks(place, mine, other_core(mine)).reshape(nrows * rows, width)
    staged = stage(after(matrix, moved))

    depth = width // nrows
    parts = local(
        product_kernel,
        (nrows, rows + depth, width),
        (y, staged, factor, col_panel, *panels),
        [pltpu.VMEM((width, nrows * rows), jnp.float32)],
    )
    parts = lax.all_to_all(parts, "row", 0, 0)
    pair = [(rows, width), (depth, width)]
    chunk, inner = local(reduce_kernel, pair, (parts,), scalars=0)

    home = lax.ppermute(chunk, ("row", "col"), to_home)
    inner = z_sum(inner)
    own_scaled = spread(after(home, inner), Z_GROUPS).reshape(block, width)
    inner = sum(y_blocks(inner))
    scaled = x_blocks(after(chunk, home))
    own_scaled = after(own_scaled, inner, *scaled)
    scaleds = y_blocks(own_scaled)

    small = x_blocks(after(inner, own_scaled))
    small += [other_core(small)]
    scaled += [other_core(scaled)]
    left, correction = middle(
        place,
        (factor, panel, home, col_panel, *scaled, *small),
        [col_panel.shape, home.shape],
        [pltpu.VMEM((nrows, size, width), jnp.float32) for size in (rows, depth)],
    )
    updated = local(
        first_update_kernel, matrix.shape, (y, staged, left, col_panel, scaleds[0], *panels)
    )
    return last_update(y, updated, scaleds[1:], col_panel), correction


def solution(mesh):
    in_specs = (P("row", "col"), P(("row", "col"), None), P())
    out_specs = (P("row", "col"), P(("row", "col"), None))
    return jax.shard_map(
        per_device, mesh=mesh, in_specs=in_specs, out_specs=out_specs, check_vma=False
    )
```

```python
import jax
import jax.numpy as jnp
from jax import lax
from jax.experimental import pallas as pl
from jax.experimental.pallas import tpu as pltpu
from jax.sharding import PartitionSpec as P

NX, NY, NZ, CORES = 4, 4, 8, 2
Z_GROUPS = [[y * NZ + z for z in range(NZ)] for y in range(NY)]
WHOLE = pl.BlockSpec(memory_space=pltpu.VMEM)
SCALARS = pl.BlockSpec(memory_space=pltpu.SMEM)
MIDDLE = 44
FREE = pl.CostEstimate(flops=1, bytes_accessed=1, transcendentals=0)
PARAMS = pltpu.CompilerParams(vmem_limit_bytes=44 << 20)


def after(value, *others):
    return lax.optimization_barrier((value,) + others)[0]


def exact(left, right, contract):
    return lax.dot_general(
        left,
        right,
        (contract, ((), ())),
        precision=lax.Precision.HIGHEST,
        preferred_element_type=jnp.float32,
    )


def halves(value):
    high = value.astype(jnp.bfloat16)
    return high, (value - high.astype(jnp.float32)).astype(jnp.bfloat16)


def three_pass(left, right, contract):
    def one(a, b):
        return lax.dot_general(a, b, (contract, ((), ())), preferred_element_type=jnp.float32)

    return one(left[0], right[1]) + one(left[1], right[0]) + one(left[0], right[0])


def spread(value, groups):
    copies = jnp.broadcast_to(value, (len(groups[0]),) + value.shape)
    return lax.all_to_all(copies, "col", 0, 0, axis_index_groups=groups)


def y_blocks(value):
    def shifted(step):
        perm = [(y * NZ + z, (y + step) % NY * NZ + z) for y in range(NY) for z in range(NZ)]
        return lax.ppermute(value, "col", perm)

    return [value] + [shifted(step) for step in range(1, NY)]


def z_sum(value):
    def partner(value, bits):
        perm = [(y * NZ + z, y * NZ + (z ^ bits)) for y in range(NY) for z in range(NZ)]
        return lax.ppermute(value, "col", perm)

    value = sum([partner(value, bits) for bits in (2, 4, 6)], value)
    return value + partner(value, 1)


def x_blocks(value):
    size = NX * CORES

    def shifted(step):
        perm = [(i, (i - CORES * step) % size) for i in range(size)]
        return lax.ppermute(value, "row", perm)

    return [value] + [shifted(step) for step in range(1, NX)]


def other_core(values):
    perm = [(i, i ^ 1) for i in range(NX * CORES)]
    return lax.ppermute(jnp.stack(values), "row", perm)


def assemble(place, mine, other, out):
    for k in range(NX):
        slot = lax.rem(place[0] + k, NX) * CORES
        out[slot + place[1]] = mine[k][...]
        out[slot + 1 - place[1]] = other[k]


def assemble_kernel(place, *refs):
    assemble(place, refs[:NX], refs[NX], refs[NX + 1])


def row_blocks(place, mine, other):
    shape = (NX * CORES,) + mine[0].shape
    return pl.pallas_call(
        assemble_kernel,
        out_shape=jax.ShapeDtypeStruct(shape, mine[0].dtype),
        in_specs=[SCALARS] + [WHOLE] * (NX + 1),
        out_specs=WHOLE,
        cost_estimate=FREE,
        compiler_params=PARAMS,
    )(place, *mine, other)


def local(kernel, shapes, operands, scratch=(), scalars=1):
    single = not isinstance(shapes, list)
    shapes = [shapes] if single else shapes
    results = pl.pallas_call(
        kernel,
        out_shape=[jax.ShapeDtypeStruct(shape, jnp.float32) for shape in shapes],
        in_specs=[SCALARS] * scalars + [WHOLE] * (len(operands) - scalars),
        out_specs=[WHOLE] * len(shapes),
        scratch_shapes=scratch,
        cost_estimate=FREE,
        compiler_params=PARAMS,
    )(*operands)
    return results[0] if single else results


def stage_kernel(matrix, out):
    pltpu.sync_copy(matrix, out)


def stage(matrix):
    return pl.pallas_call(
        stage_kernel,
        out_shape=jax.ShapeDtypeStruct(matrix.shape, matrix.dtype),
        in_specs=[pl.BlockSpec(memory_space=pl.ANY)],
        out_specs=WHOLE,
        cost_estimate=FREE,
        compiler_params=PARAMS,
    )(matrix)


def rows_of(y_ref, step, size):
    return pl.ds(pl.multiple_of(lax.rem(y_ref[0] + (NY - step), NY) * size, size), size)


def product_kernel(y_ref, matrix, factor, col_panel, *refs):
    panels, out, total = refs[:NY], refs[NY], refs[NY + 1]
    for k in range(NY):
        block = matrix[rows_of(y_ref, k, panels[k].shape[0]), :]
        piece = three_pass(halves(panels[k][...]), halves(block), ((0,), (0,)))
        if k == 0:
            total[...] = piece
        else:
            total[...] += piece
    count, rows, width = out.shape
    depth = width // count
    scaled = exact(total[...], factor[...], ((0,), (0,)))
    inner = exact(col_panel[...], scaled, ((0,), (0,)))
    out[:, : rows - depth, :] = scaled.reshape(count, rows - depth, width)
    out[:, rows - depth :, :] = inner.reshape(count, depth, width)


def reduce_kernel(parts, chunk, inner):
    total = parts[0]
    for k in range(1, parts.shape[0]):
        total += parts[k]
    chunk[...] = total[: chunk.shape[0]]
    inner[...] = total[chunk.shape[0] :]


def middle_kernel(place, factor, panel, home, col_panel, *refs):
    blocks, (left, correction, scaled, small) = refs[:-4], refs[-4:]
    half = NX + 1
    assemble(place, blocks[:NX], blocks[NX], scaled)
    assemble(place, blocks[half : half + NX], blocks[half + NX], small)
    width = panel.shape[1]
    kernel = 0.5 * exact(factor[...], small[...].reshape(width, width), ((0,), (0,)))
    correction[...] = home[...] - exact(panel[...], kernel, ((1,), (0,)))
    wanted = exact(col_panel[...], kernel + kernel.T, ((1,), (0,)))
    left[...] = scaled[...].reshape(left.shape) - wanted


def middle(place, operands, shapes, scratch):
    def whole(shape):
        return pl.BlockSpec(shape, lambda step: (0,) * len(shape))

    return pl.pallas_call(
        middle_kernel,
        out_shape=[jax.ShapeDtypeStruct(shape, jnp.float32) for shape in shapes],
        grid=(1,),
        in_specs=[SCALARS] + [whole(operand.shape) for operand in operands],
        out_specs=[whole(shape) for shape in shapes],
        scratch_shapes=scratch,
        cost_estimate=FREE,
        compiler_params=pltpu.CompilerParams(vmem_limit_bytes=MIDDLE << 20),
    )(place, *operands)


def first_update_kernel(y_ref, matrix, left, col_panel, own_scaled, *refs):
    panels, out = refs[:NY], refs[NY]
    right = halves(left[...])
    for k in range(NY):
        rows = rows_of(y_ref, k, panels[k].shape[0])
        value = matrix[rows, :] - three_pass(halves(panels[k][...]), right, ((1,), (1,)))
        if k == 0:
            pair = halves(own_scaled[...]), halves(col_panel[...])
            value -= three_pass(*pair, ((1,), (1,)))
        out[rows, :] = value


def last_update_kernel(y_ref, matrix, right, *refs):
    parts = refs[: NY - 1]
    out, right_high, right_low = refs[NY - 1 :]
    step = pl.program_id(0)

    @pl.when(step == 0)
    def _():
        right_high[...], right_low[...] = halves(right[...])
        out[...] = matrix[...]

    for k in range(1, NY):

        @pl.when(step == k)
        def _():
            pair = right_high[...], right_low[...]
            out[...] = matrix[...] - three_pass(halves(parts[k - 1][...]), pair, ((1,), (1,)))


def last_update(y, matrix, parts, right):
    rows, cols = matrix.shape
    block, width = parts[0].shape

    def moving(s, y_ref):
        return (lax.rem(y_ref[0] + (NY - s), NY), 0)

    def fixed(s, y_ref):
        return (0, 0)

    return pl.pallas_call(
        last_update_kernel,
        out_shape=jax.ShapeDtypeStruct((rows, cols), jnp.float32),
        grid_spec=pltpu.PrefetchScalarGridSpec(
            num_scalar_prefetch=1,
            grid=(NY,),
            in_specs=[pl.BlockSpec((block, cols), moving), pl.BlockSpec((cols, width), fixed)]
            + [pl.BlockSpec((block, width), fixed)] * (NY - 1),
            out_specs=pl.BlockSpec((block, cols), moving),
            scratch_shapes=[pltpu.VMEM((cols, width), jnp.bfloat16)] * 2,
        ),
        cost_estimate=FREE,
        compiler_params=PARAMS,
    )(y, matrix, right, *parts)


def per_device(matrix, panel, factor):
    nrows, ncols = lax.axis_size("row"), lax.axis_size("col")
    rows, width = panel.shape
    block = NZ * rows
    row = lax.axis_index("row")
    y = (lax.axis_index("col") // NZ).reshape(1)
    place = jnp.stack([row // CORES, row % CORES])
    total = nrows * ncols
    to_column = [(g, g % nrows * ncols + g // nrows) for g in range(total)]
    to_home = [(b, a) for a, b in to_column]

    moved = lax.ppermute(panel, ("row", "col"), to_column)
    mine = x_blocks(moved)
    panels = y_blocks(spread(panel, Z_GROUPS).reshape(block, width))
    col_panel = row_blocks(place, mine, other_core(mine)).reshape(nrows * rows, width)
    staged = stage(after(matrix, moved))

    depth = width // nrows
    parts = local(
        product_kernel,
        (nrows, rows + depth, width),
        (y, staged, factor, col_panel, *panels),
        [pltpu.VMEM((width, nrows * rows), jnp.float32)],
    )
    parts = lax.all_to_all(parts, "row", 0, 0)
    pair = [(rows, width), (depth, width)]
    chunk, inner = local(reduce_kernel, pair, (parts,), scalars=0)

    home = lax.ppermute(chunk, ("row", "col"), to_home)
    inner = z_sum(inner)
    own_scaled = spread(after(home, inner), Z_GROUPS).reshape(block, width)
    inner = sum(y_blocks(inner))
    scaled = x_blocks(after(chunk, home))
    own_scaled = after(own_scaled, inner, *scaled)
    scaleds = y_blocks(own_scaled)

    small = x_blocks(after(inner, own_scaled))
    small += [other_core(small)]
    scaled += [other_core(scaled)]
    left, correction = middle(
        place,
        (factor, panel, home, col_panel, *scaled, *small),
        [col_panel.shape, home.shape],
        [pltpu.VMEM((nrows, size, width), jnp.float32) for size in (rows, depth)],
    )
    updated = local(
        first_update_kernel, matrix.shape, (y, staged, left, col_panel, scaleds[0], *panels)
    )
    return last_update(y, updated, scaleds[1:], col_panel), correction


def solution(mesh):
    in_specs = (P("row", "col"), P(("row", "col"), None), P())
    out_specs = (P("row", "col"), P(("row", "col"), None))
    return jax.shard_map(
        per_device, mesh=mesh, in_specs=in_specs, out_specs=out_specs, check_vma=False
    )
```
